128 devices in a mesh: role: 4 (over y), fsdp: 4 (over x_hi, core), tp: 8 (over z, x_lo).
Axes of the slice: x: 4 (x_hi: 2, x_lo: 2; x = x_hi * 2 + x_lo), y: 4, z: 4, core: 2. Of those that a mesh axis runs over, the one named last changes fastest.
Arguments:
- attn_rows: bfloat16 [32768, 5120], P(('role', 'fsdp'), 'tp'), may hold values from -6 to 6
- logp_grad: bfloat16 [32768, 5120], P(('role', 'fsdp'), 'tp'), may hold values from -512 to 512
- rewards: float32 [64], P(('role', 'fsdp')), may hold values from 0 to 4
- group_ids: int32 [64], P(('role', 'fsdp')), may hold values from 0 to 5
- comp_len: int32 [64], P(('role', 'fsdp')), may hold values from 1 to 512
- o_weight: bfloat16 [5120, 5120], P(('role', 'fsdp'), 'tp'), may hold values from -0.078125 to 0.078125
- queries: bfloat16 [32, 5120], P('fsdp', 'tp'), may hold values from -200 to 200
- key_cache: bfloat16 [32, 4096, 1024], P('fsdp', None, 'tp'), may hold values from -7 to 7
- value_cache: bfloat16 [32, 4096, 1024], P('fsdp', None, 'tp'), may hold values from -96 to 96
- cache_len: int32 [32], P('fsdp'), may hold values from 2 to 4096
Outputs:
- weight_grad: float32 [5120, 5120], P(('role', 'fsdp'), 'tp')
- decode_out: bfloat16 [32, 5120], P(None, ('role', 'fsdp'))
The draws below stay inside these ranges and needn't reach their ends.
All inputs are finite; a program needn't handle non-finite values.
Results may differ from the reference program's by a relative error of at most 0.0057.
Values may be sent and summed in bfloat16 or wider, within the bound.
No kernel may reach another device: no remote copies, remote signals or barrier semaphores. Data moves between devices by JAX's collectives and lax.ppermute only.
A program may use at most 192 MiB of HBM per device.

```python
import math
import jax
import jax.numpy as jnp
from jax import lax

D = 5120
HEADS = 40
KV_HEADS = 8
HEAD_DIM = 128
COMP_TOKENS = 512
GROUPS = 6
SEQ_DEV = 4
CACHE = 4096
COMPLETIONS = 64
ROWS = 32768
SEQS = 32
N_ROLE = 4
N_FSDP = 4


def shared_heads(key):
    key_rows = jnp.clip(jax.random.normal(jax.random.fold_in(key, 11), (SEQS, CACHE, KV_HEADS * HEAD_DIM), jnp.float32), -6.0, 6.0)
    query_rows = jnp.clip(jax.random.normal(jax.random.fold_in(key, 13), (SEQS, HEADS * HEAD_DIM), jnp.float32), -6.0, 6.0)
    return (query_rows, key_rows)


def draw_queries(key, part):
    return shared_heads(key)[0].astype(jnp.bfloat16)


def draw_key_cache(key, part):
    return shared_heads(key)[1].astype(jnp.bfloat16)


def plant(drawn, key, low, largest):
    extent = drawn.shape
    place = [jax.random.randint(jax.random.fold_in(key, axis), (), 0, extent[axis]) for axis in range(len(extent))]
    drawn = drawn.at[tuple(place)].set(low)
    longest = extent.index(max(extent))
    place[longest] = (place[longest] + 1) % extent[longest]
    return drawn.at[tuple(place)].set(largest)


def spiked(array, key, source, target, shards_of, factor):
    owner, partner = [(jnp.arange(array.shape[dim]) // (array.shape[dim] // shards_of)).reshape([-1 if axis == dim else 1 for axis in range(array.ndim)]) for dim in (source, target)]
    chosen = jax.random.permutation(key, shards_of)[partner]
    strong = (owner == chosen) | (owner == (partner + shards_of // 2) % shards_of)
    return jnp.where(strong, factor * array, array)


def steps_of(rng, dims, shards, low, high):
    loudness = 1.0
    for position, blocks in shards:
        steps = jax.random.uniform(jax.random.fold_in(jax.random.fold_in(rng, 6), position), (blocks,), jnp.float32, low / len(shards), high / len(shards))
        loudness = loudness * jnp.repeat(jnp.exp(steps), dims[position] // blocks).reshape((-1,) + (1,) * (len(dims) - 1 - position))
    return loudness


def noise(key, shape, scale, reach, pieces=(), dtype=jnp.bfloat16):
    drawn = scale * jax.random.normal(key, shape, jnp.float32)
    if pieces:
        drawn = drawn * steps_of(key, shape, pieces, -0.22, 0.18)
    return jnp.clip(drawn, -reach, reach).astype(dtype)


def heavy_noise(own_key, shape, scale, bound, pieces, heavy, kind=jnp.bfloat16):
    drawn = scale * jax.random.normal(own_key, shape, jnp.float32)
    if pieces:
        drawn = drawn * steps_of(own_key, shape, pieces, -0.22, 0.18)
    return jnp.clip(spiked(drawn, jax.random.fold_in(own_key, 3), *heavy), -bound, bound).astype(kind)


def setup_inputs(seed: int = 0) -> dict:
    keys = jax.random.split(jax.random.key(seed), 11)
    attn_rows = noise(keys[0], (ROWS, HEADS * HEAD_DIM), 1.0, 6.0, ((0, 16), (1, 8)))
    logp_grad = heavy_noise(keys[1], (ROWS, D), 64.0, 512.0, ((0, 16), (1, 8)), (0, 1, 16, 2.0))
    rewards = jnp.clip(4.0 * jax.random.uniform(keys[2], (COMPLETIONS,), jnp.float32) ** steps_of(keys[2], (COMPLETIONS,), ((0, 16),), -0.2, 0.2), 0.0, 4.0)
    group_ids = plant(jax.random.randint(keys[3], (COMPLETIONS,), 0, GROUPS), jax.random.fold_in(keys[3], 1), 0, GROUPS - 1).astype(jnp.int32)
    comp_len = plant(jax.random.randint(keys[4], (COMPLETIONS,), 1, COMP_TOKENS + 1), jax.random.fold_in(keys[4], 1), 1, COMP_TOKENS).astype(jnp.int32)
    o_weight = noise(keys[5], (D, HEADS * HEAD_DIM), (HEADS * HEAD_DIM) ** -0.5, 0.078125, ((0, 16), (1, 8)))
    queries = draw_queries(jax.random.fold_in(keys[10], 71), 0)
    key_cache = draw_key_cache(jax.random.fold_in(keys[10], 71), 0)
    value_cache = noise(keys[8], (SEQS, CACHE, KV_HEADS * HEAD_DIM), 16.0, 96.0, ((0, 4), (2, 8)))
    cache_len = plant(jax.random.randint(keys[9], (SEQS,), 2, CACHE + 1), jax.random.fold_in(keys[9], 1), 2, CACHE).astype(jnp.int32)
    return dict(attn_rows=attn_rows, logp_grad=logp_grad, rewards=rewards, group_ids=group_ids, comp_len=comp_len, o_weight=o_weight, queries=queries, key_cache=key_cache, value_cache=value_cache, cache_len=cache_len)


def group_advantage(rewards, group_ids, tallies, reward_sums, square_sums):
    member = (group_ids[:, None] == jnp.arange(GROUPS)[None, :]).astype(jnp.float32)
    divisor = jnp.maximum(tallies, 1.0)
    group_mean = reward_sums / divisor
    group_spread = jnp.sqrt(jnp.maximum(square_sums / divisor - group_mean * group_mean, 0.0))
    row_mean = lax.optimization_barrier(jnp.sum(member * group_mean[None, :], axis=1))
    row_spread = lax.optimization_barrier(jnp.sum(member * group_spread[None, :], axis=1))
    return (rewards - row_mean) / jnp.maximum(row_spread, 1.0)

def reference(attn_rows, logp_grad, rewards, group_ids, comp_len, o_weight, queries, key_cache, value_cache, cache_len):
    learner_count = (N_ROLE - 1) * N_FSDP * SEQ_DEV
    live = (jnp.arange(COMPLETIONS) < learner_count).astype(jnp.float32)
    member = (group_ids[:, None] == jnp.arange(GROUPS)[None, :]).astype(jnp.float32) * live[:, None]
    tallies = lax.optimization_barrier(jnp.sum(member, axis=0))
    reward_sums = lax.optimization_barrier(jnp.sum(member * rewards[:, None], axis=0))
    square_sums = lax.optimization_barrier(jnp.sum(member * (rewards * rewards)[:, None], axis=0))
    live_tokens = jnp.sum(live * comp_len.astype(jnp.float32))
    advantage = group_advantage(rewards, group_ids, tallies, reward_sums, square_sums)
    inside = (jnp.arange(COMP_TOKENS)[None, :] < comp_len[:, None]).astype(jnp.float32)
    row_scale = (advantage[:, None] * inside * live[:, None] / live_tokens).reshape(ROWS)
    token_grads = (logp_grad.astype(jnp.float32) * row_scale[:, None]).astype(jnp.bfloat16)
    used_rows = learner_count * COMP_TOKENS
    weight_grad = jnp.dot(token_grads[:used_rows].astype(jnp.float32).T, attn_rows[:used_rows].astype(jnp.float32), precision=lax.Precision.HIGHEST)
    per_group = HEADS // KV_HEADS
    query_heads = queries.astype(jnp.float32).reshape(SEQS, KV_HEADS, per_group, HEAD_DIM)
    key_heads = key_cache.astype(jnp.float32).reshape(SEQS, CACHE, KV_HEADS, HEAD_DIM)
    scores = jnp.einsum('skgd,sckd->skgc', query_heads, key_heads) / math.sqrt(HEAD_DIM)
    filled = jnp.arange(CACHE)[None, :] < cache_len[:, None]
    scores = jnp.where(filled[:, None, None, :], scores, -jnp.inf)
    highest = lax.optimization_barrier(jnp.max(scores, axis=-1, keepdims=True))
    raised = jnp.exp(scores - highest)
    attn_weights = (raised / lax.optimization_barrier(jnp.sum(raised, axis=-1, keepdims=True))).astype(jnp.bfloat16)
    value_heads = value_cache.astype(jnp.float32).reshape(SEQS, CACHE, KV_HEADS, HEAD_DIM)
    mixed = jnp.einsum('skgc,sckd->skgd', attn_weights.astype(jnp.float32), value_heads).astype(jnp.bfloat16)
    mixed = mixed.reshape(SEQS, HEADS * HEAD_DIM)
    decode_out = jnp.dot(mixed, o_weight.T, preferred_element_type=jnp.float32).astype(jnp.bfloat16)
    return (weight_grad, decode_out)
```

```python
import math

import jax
import jax.numpy as jnp
from jax import lax
from jax.sharding import PartitionSpec as P

HEADS = 40
KV_HEADS = 8
HEAD_DIM = 128
COMP_TOKENS = 512
GROUPS = 6
AXES = ("role", "fsdp", "tp")


def device_index(y, xh, c, z, xl):
    return ((y * 2 + xh) * 2 + c) * 8 + z * 2 + xl


def pairs_of(target):
    pairs = []
    for y in range(4):
        for xh in range(2):
            for c in range(2):
                for z in range(4):
                    for xl in range(2):
                        to = target(y, xh, c, z, xl)
                        if to is not None:
                            pairs.append((device_index(y, xh, c, z, xl), device_index(*to)))
    return pairs


def send(value, target):
    return lax.ppermute(value, AXES, pairs_of(target))


def exchange_sum(value, targets):
    for target in targets:
        value = value + send(value, target)
    return value


def over_ring(c, z, step):
    return (z + step) % 4 if c == 0 else (z - step) % 4


def learner(target):
    return lambda y, xh, c, z, xl: target(y, xh, c, z, xl) if y < 3 else None


def group_advantage(rewards, group_ids, tallies, reward_sums, square_sums):
    member = (group_ids[:, None] == jnp.arange(GROUPS)[None, :]).astype(jnp.float32)
    divisor = jnp.maximum(tallies, 1.0)
    group_mean = reward_sums / divisor
    group_spread = jnp.sqrt(jnp.maximum(square_sums / divisor - group_mean * group_mean, 0.0))
    row_mean = jnp.sum(member * group_mean[None, :], axis=1)
    row_spread = jnp.sum(member * group_spread[None, :], axis=1)
    return (rewards - row_mean) / jnp.maximum(row_spread, 1.0)


def attend(queries, key_cache, value_cache, cache_len):
    seq_count = queries.shape[0]
    slot_count = key_cache.shape[1]
    kv_local = key_cache.shape[2] // HEAD_DIM
    per_group = HEADS // KV_HEADS
    query_heads = queries.reshape(seq_count, kv_local, per_group, HEAD_DIM)
    key_heads = key_cache.reshape(seq_count, slot_count, kv_local, HEAD_DIM)
    scores = jnp.einsum(
        "skgd,sckd->skgc", query_heads, key_heads, preferred_element_type=jnp.float32
    ) / math.sqrt(HEAD_DIM)
    filled = jnp.arange(slot_count)[None, :] < cache_len[:, None]
    scores = jnp.where(filled[:, None, None, :], scores, -jnp.inf)
    highest = jnp.max(scores, axis=-1, keepdims=True)
    raised = jnp.exp(scores - highest)
    attn_weights = (raised / jnp.sum(raised, axis=-1, keepdims=True)).astype(jnp.bfloat16)
    value_heads = value_cache.reshape(seq_count, slot_count, kv_local, HEAD_DIM)
    mixed = jnp.einsum(
        "skgc,sckd->skgd", attn_weights, value_heads, preferred_element_type=jnp.float32
    )
    return mixed.astype(jnp.bfloat16).reshape(seq_count, kv_local * per_group * HEAD_DIM)


def row_scales(rewards, group_ids, comp_len):
    role_index = lax.axis_index("role")
    live = (role_index < lax.axis_size("role") - 1).astype(jnp.float32)
    member = (group_ids[:, None] == jnp.arange(GROUPS)[None, :]).astype(jnp.float32) * live
    stats = jnp.stack(
        (
            jnp.sum(member, axis=0),
            jnp.sum(member * rewards[:, None], axis=0),
            jnp.sum(member * (rewards * rewards)[:, None], axis=0),
            jnp.full((GROUPS,), jnp.sum(comp_len.astype(jnp.float32)) * live),
        )
    )
    stats = exchange_sum(
        stats,
        (
            lambda y, xh, c, z, xl: (y, xh, 1 - c, z, xl),
            lambda y, xh, c, z, xl: (y ^ 1, xh, c, z, xl),
            lambda y, xh, c, z, xl: (y ^ 2, xh, c, z, xl),
            lambda y, xh, c, z, xl: (y, 1 - xh, c, z, xl),
        ),
    )
    advantage = group_advantage(rewards, group_ids, stats[0], stats[1], stats[2])
    inside = (jnp.arange(COMP_TOKENS)[None, :] < comp_len[:, None]).astype(jnp.float32)
    return (advantage[:, None] * inside * live / stats[3, 0]).reshape(-1)


def local(
    attn_rows,
    logp_grad,
    rewards,
    group_ids,
    comp_len,
    o_weight,
    queries,
    key_cache,
    value_cache,
    cache_len,
):
    y = lax.axis_index("role")
    xh = lax.axis_index("fsdp") // 2
    c = lax.axis_index("fsdp") % 2
    z = lax.axis_index("tp") // 2
    xl = lax.axis_index("tp") % 2
    half = logp_grad.shape[1] // 2
    first = c == 0

    low, high = logp_grad[:, :half].T, logp_grad[:, half:].T
    keep = jnp.where(first, low, high)
    give = jnp.where(first, high, low)
    rows_own = attn_rows
    rows_other = send(attn_rows, learner(lambda y, xh, c, z, xl: (y, xh, c, z, 1 - xl)))
    keeps, gives = [keep], [give]
    for _ in range(3):
        keeps.append(
            send(keeps[-1], learner(lambda y, xh, c, z, xl: (y, xh, c, over_ring(c, z, 1), xl)))
        )
        gives.append(
            send(gives[-1], learner(lambda y, xh, c, z, xl: (y, xh, c, over_ring(c, z, -1), xl)))
        )
    scale = row_scales(rewards, group_ids, comp_len)

    def product(piece, rows):
        grads = (piece.astype(jnp.float32) * scale[None, :]).astype(jnp.bfloat16)
        return lax.dot_general(
            grads, rows, (((1,), (0,)), ((), ())), preferred_element_type=jnp.float32
        )

    def swap_core(y, xh, c, z, xl):
        return (y, xh, 1 - c, z, xl)

    def reduced(rows):
        total = None
        for step in range(4):
            given = send(product(gives[step], rows).astype(jnp.bfloat16), learner(swap_core))
            kept = product(keeps[step], rows) + given.astype(jnp.float32)
            kept = kept.astype(jnp.bfloat16)
            owner = jnp.where(first, (z - step) % 4, (z + step) % 4)
            terms = jnp.where((owner == y) & (y < 3), kept, 0).astype(jnp.float32)
            for source in range(3):

                def to_owner(y, xh, c, z, xl, source=source, step=step):
                    to = over_ring(c, z, -step)
                    return (to, xh, c, z, xl) if y == source and to != y else None

                terms = terms + send(kept, to_owner).astype(jnp.float32)
            total = terms if total is None else total + terms
        return total

    sum_own = reduced(rows_own)
    sum_other = reduced(rows_other)
    same = xh == xl
    outgoing = jnp.where(same, sum_other, sum_own).astype(jnp.bfloat16)
    one = send(
        outgoing,
        lambda y, xh, c, z, xl: (y, xh, c, z, 1 - xl) if xh == xl else (y, xl, c, z, xl),
    )
    two = send(
        sum_other.astype(jnp.bfloat16),
        lambda y, xh, c, z, xl: None if xh == xl else (y, xl, c, z, 1 - xl),
    )
    weight_grad = (
        jnp.where(same, sum_own, 0.0) + one.astype(jnp.float32) + two.astype(jnp.float32)
    )

    own_heads = attend(queries, key_cache, value_cache, cache_len)
    all_heads = lax.all_gather(own_heads, "fsdp", axis=0, tiled=True)
    partial_out = lax.dot_general(
        all_heads, o_weight, (((1,), (1,)), ((), ())), preferred_element_type=jnp.float32
    )
    decode_out = exchange_sum(
        partial_out,
        (
            lambda y, xh, c, z, xl: (y, xh, c, z, 1 - xl),
            lambda y, xh, c, z, xl: (y, xh, c, z ^ 1, xl),
            lambda y, xh, c, z, xl: (y, xh, c, z ^ 2, xl),
        ),
    ).astype(jnp.bfloat16)
    return (weight_grad, decode_out)


def solution(mesh):
    in_specs = (
        P(("role", "fsdp"), "tp"),
        P(("role", "fsdp"), "tp"),
        P(("role", "fsdp")),
        P(("role", "fsdp")),
        P(("role", "fsdp")),
        P(("role", "fsdp"), "tp"),
        P("fsdp", "tp"),
        P("fsdp", None, "tp"),
        P("fsdp", None, "tp"),
        P("fsdp"),
    )
    out_specs = (P(("role", "fsdp"), "tp"), P(None, ("role", "fsdp")))
    return jax.shard_map(local, mesh=mesh, in_specs=in_specs, out_specs=out_specs, check_vma=False)
```

```python
import functools
import math

import jax
import jax.numpy as jnp
from jax import lax
from jax.experimental import pallas as pl
from jax.experimental.pallas import tpu as pltpu
from jax.sharding import PartitionSpec as P


HEADS = 40
KV_HEADS = 8
HEAD_DIM = 128
COMP_TOKENS = 512
GROUPS = 6
AXES = ("role", "fsdp", "tp")
PHASES = (((128, 512),), ((0, 128), (512, 640)))


def device_index(y, xh, c, z, xl):
    return ((y * 2 + xh) * 2 + c) * 8 + z * 2 + xl


def pairs_of(target):
    pairs = []
    for y in range(4):
        for xh in range(2):
            for c in range(2):
                for z in range(4):
                    for xl in range(2):
                        to = target(y, xh, c, z, xl)
                        if to is not None:
                            pairs.append((device_index(y, xh, c, z, xl), device_index(*to)))
    return pairs


def send(value, target):
    return lax.ppermute(value, AXES, pairs_of(target))


def learner(target):
    return lambda y, xh, c, z, xl: target(y, xh, c, z, xl) if y < 3 else None


def group_advantage(rewards, group_ids, tallies, reward_sums, square_sums):
    member = (group_ids[:, None] == jnp.arange(GROUPS)[None, :]).astype(jnp.float32)
    divisor = jnp.maximum(tallies, 1.0)
    group_mean = reward_sums / divisor
    group_spread = jnp.sqrt(jnp.maximum(square_sums / divisor - group_mean * group_mean, 0.0))
    row_mean = jnp.sum(member * group_mean[None, :], axis=1)
    row_spread = jnp.sum(member * group_spread[None, :], axis=1)
    return (rewards - row_mean) / jnp.maximum(row_spread, 1.0)


def attend(queries, key_cache, value_cache, cache_len):
    seq_count = queries.shape[0]
    slot_count = key_cache.shape[1]
    kv_local = key_cache.shape[2] // HEAD_DIM
    per_group = HEADS // KV_HEADS
    query_heads = queries.reshape(seq_count, kv_local, per_group, HEAD_DIM)
    key_heads = key_cache.reshape(seq_count, slot_count, kv_local, HEAD_DIM)
    scores = jnp.einsum(
        "skgd,sckd->skgc", query_heads, key_heads, preferred_element_type=jnp.float32
    ) / math.sqrt(HEAD_DIM)
    filled = jnp.arange(slot_count)[None, :] < cache_len[:, None]
    scores = jnp.where(filled[:, None, None, :], scores, -jnp.inf)
    highest = jnp.max(scores, axis=-1, keepdims=True)
    raised = jnp.exp(scores - highest)
    attn_weights = (raised / jnp.sum(raised, axis=-1, keepdims=True)).astype(jnp.bfloat16)
    value_heads = value_cache.reshape(seq_count, slot_count, kv_local, HEAD_DIM)
    mixed = jnp.einsum(
        "skgc,sckd->skgd", attn_weights, value_heads, preferred_element_type=jnp.float32
    )
    return mixed.astype(jnp.bfloat16).reshape(seq_count, kv_local * per_group * HEAD_DIM)


def turn_kernel(spans, grad_ref, *turned_refs):
    grads = grad_ref[...].T
    half = turned_refs[0].shape[0]
    row = 0
    for start, stop in spans:
        while start < stop:
            part, offset = divmod(row, half)
            size = min(stop - start, half - offset)
            turned_refs[part][offset : offset + size, :] = grads[start : start + size]
            start += size
            row += size


def turned(number, logp_grad):
    count, columns = logp_grad.shape
    half = sum(stop - start for start, stop in PHASES[number]) // 2
    shape = jax.ShapeDtypeStruct((half, count), jnp.bfloat16)
    return pl.pallas_call(
        functools.partial(turn_kernel, PHASES[number]),
        grid=(count // COMP_TOKENS,),
        out_shape=(shape, shape),
        in_specs=[pl.BlockSpec((COMP_TOKENS, columns), lambda i: (i, 0))],
        out_specs=[pl.BlockSpec((half, COMP_TOKENS), lambda i: (0, i))] * 2,
        cost_estimate=pl.CostEstimate(
            flops=0, bytes_accessed=4 * count * columns, transcendentals=0
        ),
    )(logp_grad)


def scaled_into(grads_ref, row, piece_ref, lens_ref, scales_ref):
    height = piece_ref.shape[0]
    for completion in range(piece_ref.shape[1] // COMP_TOKENS):
        span = slice(completion * COMP_TOKENS, (completion + 1) * COMP_TOKENS)
        slot = lax.broadcasted_iota(jnp.int32, (1, COMP_TOKENS), 1)
        scale = jnp.where(slot < lens_ref[completion], scales_ref[completion], 0.0)
        grads = piece_ref[:, span].astype(jnp.float32) * scale
        grads_ref[row : row + height, span] = grads.astype(jnp.bfloat16)


def halves_of(place_ref, half, block):
    mine = pl.multiple_of((2 * block + place_ref[0]) * half, half)
    theirs = pl.multiple_of((2 * block + 1 - place_ref[0]) * half, half)
    return pl.ds(mine, half), pl.ds(theirs, half)


def store_block(place_ref, total_ref, block, slot, keep_ref, give_ref):
    mine, theirs = halves_of(place_ref, keep_ref.shape[1], block)
    keep_ref[slot] = total_ref[mine, :].astype(jnp.bfloat16)
    give_ref[slot] = total_ref[theirs, :].astype(jnp.bfloat16)


def own_kernel(place_ref, lens_ref, scales_ref, *refs):
    pieces, own_ref = refs[:6], refs[6]
    keep_ref, give_ref, grads_ref, total_ref = refs[7:]
    half = pieces[0].shape[0]
    for number, piece_ref in enumerate(pieces):
        scaled_into(grads_ref, number * half, piece_ref, lens_ref, scales_ref)
    total_ref[...] = jnp.dot(grads_ref[...], own_ref[...], preferred_element_type=jnp.float32)
    for block in range(3):
        store_block(place_ref, total_ref, block, place_ref[1 + block], keep_ref, give_ref)


def rest_kernel(place_ref, lens_ref, scales_ref, *refs):
    pieces, own_ref, other_ref = refs[:8], refs[8], refs[9]
    keep_ref, give_ref, grads_ref, total_ref = refs[10:]
    half = pieces[0].shape[0]
    for number, piece_ref in enumerate(pieces):
        scaled_into(grads_ref, number * half, piece_ref, lens_ref, scales_ref)
    total_ref[...] = jnp.dot(grads_ref[...], other_ref[...], preferred_element_type=jnp.float32)
    for block in range(4):
        store_block(place_ref, total_ref, block, place_ref[1 + block], keep_ref, give_ref)
    far = slice(6 * half, 8 * half)
    total_ref[far, :] = jnp.dot(
        grads_ref[far, :], own_ref[...], preferred_element_type=jnp.float32
    )
    store_block(place_ref, total_ref, 3, 4, keep_ref, give_ref)


def outer_call(kernel, scalars, pieces, rows, shape):
    height = sum(piece.shape[0] for piece in pieces)
    count = pieces[0].shape[1]
    columns = shape[-1]
    smem = pl.BlockSpec(memory_space=pltpu.SMEM)
    vmem = pl.BlockSpec(memory_space=pltpu.VMEM)
    out = jax.ShapeDtypeStruct(shape, jnp.bfloat16)
    return pl.pallas_call(
        kernel,
        out_shape=(out, out),
        in_specs=[smem] * len(scalars) + [vmem] * (len(pieces) + len(rows)),
        out_specs=(vmem, vmem),
        scratch_shapes=[
            pltpu.VMEM((height, count), jnp.bfloat16),
            pltpu.VMEM((height, columns), jnp.float32),
        ],
        compiler_params=pltpu.CompilerParams(vmem_limit_bytes=44 * 1024 * 1024),
        cost_estimate=pl.CostEstimate(
            flops=2 * count * height * columns,
            bytes_accessed=2 * count * (height + columns) + 4 * height * columns,
            transcendentals=0,
        ),
    )(*scalars, *pieces, *rows)


def sum_kernel(place_ref, keep_own_ref, given_own_ref, keep_ref, given_ref, *sum_refs):
    columns = keep_ref.shape[2]
    for shift, sum_ref in enumerate(sum_refs):
        own = keep_own_ref[shift].astype(jnp.float32) + given_own_ref[shift].astype(jnp.float32)
        other = keep_ref[shift].astype(jnp.float32) + given_ref[shift].astype(jnp.float32)
        far = keep_ref[4].astype(jnp.float32) + given_ref[4].astype(jnp.float32)
        own = jnp.where(place_ref[4] == shift, far, own)
        sum_ref[:, :columns] = own.astype(sum_ref.dtype)
        sum_ref[:, columns:] = other.astype(sum_ref.dtype)


def sums_of(place, keep_own, given_own, keep, given):
    shape = (keep.shape[1], 2 * keep.shape[2])
    kinds = (jnp.float32, jnp.bfloat16, jnp.bfloat16, jnp.bfloat16)
    vmem = pl.BlockSpec(memory_space=pltpu.VMEM)
    return pl.pallas_call(
        sum_kernel,
        out_shape=[jax.ShapeDtypeStruct(shape, kind) for kind in kinds],
        in_specs=[pl.BlockSpec(memory_space=pltpu.SMEM)] + [vmem] * 4,
        out_specs=[vmem] * 4,
        compiler_params=pltpu.CompilerParams(vmem_limit_bytes=20 * 1024 * 1024),
        cost_estimate=pl.CostEstimate(
            flops=8 * keep.size, bytes_accessed=10 * keep.size, transcendentals=0
        ),
    )(place, keep_own, given_own, keep, given)


def local_stats(rewards, group_ids, comp_len, live):
    member = (group_ids[:, None] == jnp.arange(GROUPS)[None, :]).astype(jnp.float32) * live
    return jnp.concatenate(
        (
            jnp.sum(member, axis=0),
            jnp.sum(member * rewards[:, None], axis=0),
            jnp.sum(member * (rewards * rewards)[:, None], axis=0),
            jnp.sum(comp_len.astype(jnp.float32), keepdims=True) * live,
        )
    )


def body(
    attn_rows,
    logp_grad,
    rewards,
    group_ids,
    comp_len,
    o_weight,
    queries,
    key_cache,
    value_cache,
    cache_len,
):
    y = lax.axis_index("role")
    xh = lax.axis_index("fsdp") // 2
    c = lax.axis_index("fsdp") % 2
    z = lax.axis_index("tp") // 2
    xl = lax.axis_index("tp") % 2
    same = xh == xl
    columns = attn_rows.shape[1]
    place = jnp.stack([c] + [(z + d - y) % 4 for d in (0, -1, 1, 2)]).astype(jnp.int32)

    def up(y, xh, c, z, xl):
        return (y, xh, c, (z + 1) % 4, xl)

    def other_core(y, xh, c, z, xl):
        return (y, xh, 1 - c, z, xl)

    def down(y, xh, c, z, xl):
        return (y, xh, c, (z - 1) % 4, xl)

    rows_other = send(attn_rows, lambda y, xh, c, z, xl: (y, xh, c, z, 1 - xl))
    gathered = []
    for number in range(len(PHASES)):
        here = turned(number, logp_grad)
        behind = [send(here[part], up) for part in range(2)]
        ahead = [send(here[part], down) for part in range(2)]
        far = (send(behind[0], up), send(ahead[1], down))
        gathered.append(((*here, *behind, *ahead), far))

    seqs = queries.shape[0] // 4

    def own(array):
        return lax.dynamic_slice_in_dim(array, y * seqs, seqs, axis=0)

    heads = attend(own(queries), own(key_cache), own(value_cache), own(cache_len))
    live = (y < 3).astype(jnp.float32)
    stats = local_stats(rewards, group_ids, comp_len, live)
    everyone = jnp.concatenate(
        (heads.astype(jnp.float32), jnp.pad(stats, (0, columns - stats.shape[0]))[None])
    )[None]
    exchanges = (
        (c, lambda y, xh, c, z, xl: (y, xh, 1 - c, z, xl)),
        (y % 2, lambda y, xh, c, z, xl: (y ^ 1, xh, c, z, xl)),
        (y // 2, lambda y, xh, c, z, xl: (y ^ 2, xh, c, z, xl)),
    )
    for bit, target in exchanges:
        theirs = send(everyone, target)
        everyone = jnp.where(
            bit == 0,
            jnp.concatenate((everyone, theirs)),
            jnp.concatenate((theirs, everyone)),
        )
    totals = jnp.sum(everyone[:, seqs, : stats.shape[0]], axis=0)
    totals = totals + send(totals, lambda y, xh, c, z, xl: (y, 1 - xh, c, z, 1 - xl))
    advantage = group_advantage(
        rewards, group_ids, totals[:GROUPS], totals[GROUPS : 2 * GROUPS], totals[2 * GROUPS : -1]
    )
    scales = advantage * live / totals[-1]
    heads = everyone[:, :seqs].astype(jnp.bfloat16)
    theirs = send(heads, lambda y, xh, c, z, xl: (y, 1 - xh, c, z, xl))
    heads = jnp.where(xh == 0, jnp.stack((heads, theirs)), jnp.stack((theirs, heads)))
    all_heads = heads.reshape(2, 4, 2, seqs, columns).swapaxes(1, 2).reshape(-1, columns)
    decode_out = lax.dot_general(
        all_heads, o_weight, (((1,), (1,)), ((), ())), preferred_element_type=jnp.float32
    )
    partners = (
        lambda y, xh, c, z, xl: (y, xh, c, z, 1 - xl),
        lambda y, xh, c, z, xl: (y, xh, c, z ^ 1, xl),
        lambda y, xh, c, z, xl: (y, xh, c, z ^ 2, xl),
    )
    for target in partners:
        decode_out = decode_out + send(decode_out, target)
    decode_out = decode_out.astype(jnp.bfloat16)

    finished = []
    for near, far in gathered:
        scalars = (place, comp_len, scales)
        half = near[0].shape[0]
        keep_own, give_own = outer_call(own_kernel, scalars, near, (attn_rows,), (4, half, columns))
        given_own = send(give_own, other_core)
        keep, give = outer_call(
            rest_kernel, scalars, (*near, *far), (attn_rows, rows_other), (5, half, columns)
        )
        given = send(give, other_core)
        sums = sums_of(place, keep_own, given_own, keep, given)
        parts = [
            send(
                sums[shift],
                learner(lambda y, xh, c, z, xl, shift=shift: ((y + shift) % 4, xh, c, z, xl)),
            )
            for shift in range(1, 4)
        ]
        total = sums[0]
        for part in parts:
            total = total + part.astype(jnp.float32)
        sum_own, sum_other = total[:, :columns], total[:, columns:]
        one = send(
            jnp.where(same, sum_other, sum_own).astype(jnp.bfloat16),
            lambda y, xh, c, z, xl: (y, xh, c, z, 1 - xl) if xh == xl else (y, xl, c, z, xl),
        )
        two = send(
            sum_other.astype(jnp.bfloat16),
            lambda y, xh, c, z, xl: None if xh == xl else (y, xl, c, z, 1 - xl),
        )
        finished.append(
            jnp.where(same, sum_own, 0.0) + one.astype(jnp.float32) + two.astype(jnp.float32)
        )
    weight_grad = jnp.where(c == 0, jnp.concatenate(finished[::-1]), jnp.concatenate(finished))
    return (weight_grad, decode_out)


def solution(mesh):
    in_specs = (
        P(("role", "fsdp"), "tp"),
        P(("role", "fsdp"), "tp"),
        P(("role", "fsdp")),
        P(("role", "fsdp")),
        P(("role", "fsdp")),
        P(("role", "fsdp"), "tp"),
        P("fsdp", "tp"),
        P("fsdp", None, "tp"),
        P("fsdp", None, "tp"),
        P("fsdp"),
    )
    out_specs = (P(("role", "fsdp"), "tp"), P(None, ("role", "fsdp")))
    return jax.shard_map(body, mesh=mesh, in_specs=in_specs, out_specs=out_specs, check_vma=False)
```
